32 devices in a mesh: sub: 4 (over y, x), blk: 8 (over z, core).
Axes of the slice: x: 2, y: 2, z: 4, core: 2. Of those that a mesh axis runs over, the one named last changes fastest.
Arguments:
- schur: bfloat16 [4, 8192, 8192], P('sub', 'blk'), as said below
- inverse_blocks: float32 [4, 64, 128, 128], P('sub', 'blk'), as said below
- loads: float32 [4, 32, 8192], P('sub', None, 'blk'), may hold values from -6 to 6
- share_list: int32 [4, 4, 4], P('sub'), may hold values from -1 to 63, as said below
- multiplicity: int32 [4, 64], P('sub', 'blk'), may hold values from 1 to 2, as said below
Outputs:
- solution: float32 [4, 32, 8192], P('sub', None, 'blk')
- misfit: float32 [32, 96], replicated
The draws below stay inside these ranges and needn't reach their ends.
Inputs may be any that keep to these rules, and one draw needn't show every extreme that they name: share_list[i, j, s] is the local block of subdomain i that holds the s-th block it shares with subdomain j, or -1 for an empty slot; share_list[j, i, s] is the same block in the numbering of j; the used slots of a pair come first and are as many both ways; share_list[i, i, :] is -1; no block of a subdomain appears twice in its list; at most 4 blocks a pair. multiplicity[i, k] is 2 where block k of subdomain i appears in share_list[i], else 1. `schur`: each local Schur complement is a full dense matrix. `inverse_blocks`: full dense blocks.
All inputs are finite; a program needn't handle non-finite values.
Results may differ from the reference program's by a relative error of at most 0.0026.
Values may be sent and summed in bfloat16 or wider, within the bound.
No kernel may reach another device: no remote copies, remote signals or barrier semaphores. Data moves between devices by JAX's collectives and lax.ppermute only.
A program may use at most 64 MiB of HBM per device.

```python
import math
import jax
import jax.numpy as jnp
from jax import lax

ORDER = 8192
BLOCK = 128
SLOTS = 4
CASES = 32
ITERS = 2
NSUBS = 4
BLOCKS = 64


def interface_tables(key):
    base = jax.random.fold_in(key, 7)
    counts = jax.random.randint(jax.random.fold_in(base, 1), (NSUBS, NSUBS), 0, SLOTS + 1)
    counts = jnp.triu(counts, 1)
    counts = counts + counts.T
    busiest = jax.random.randint(jax.random.fold_in(base, 2), (), 0, NSUBS)
    ident = jnp.arange(NSUBS, dtype=jnp.int32)
    touched = (ident[:, None] == busiest) | (ident[None, :] == busiest)
    offdiag = ident[:, None] != ident[None, :]
    counts = jnp.where(touched & offdiag, SLOTS, counts)
    orders = jax.vmap(lambda which: jax.random.permutation(jax.random.fold_in(base, 100 + which), BLOCKS))(ident)
    slot_ids = jnp.arange(SLOTS, dtype=jnp.int32)
    ranked = ident[None, :] - (ident[None, :] > ident[:, None]).astype(jnp.int32)
    position = jnp.minimum(ranked[:, :, None] * SLOTS + slot_ids[None, None, :], BLOCKS - 1)
    chosen = orders[ident[:, None, None], position]
    valid = (slot_ids[None, None, :] < counts[:, :, None]) & offdiag[:, :, None]
    shared = jnp.where(valid, chosen, -1).astype(jnp.int32)
    present = jnp.any(shared[:, :, :, None] == jnp.arange(BLOCKS, dtype=jnp.int32)[None, None, None, :], axis=(1, 2))
    return (shared, (1 + present.astype(jnp.int32)).astype(jnp.int32))


def draw_share_list(key, part):
    return interface_tables(key)[0]


def draw_multiplicity(key, part):
    return interface_tables(key)[1]


def draw_schur(key, part):

    def single(which):
        sub_key = jax.random.fold_in(key, which)
        noise = jax.random.normal(sub_key, (ORDER, ORDER), jnp.float32)
        diagonal = jnp.ones((ORDER,), jnp.float32)
        symmetric = (noise + noise.T) * (0.3 / math.sqrt(2.0 * ORDER))
        return (jnp.diag(diagonal) + symmetric).astype(jnp.bfloat16)
    return lax.map(single, jnp.arange(NSUBS, dtype=jnp.int32))


def draw_inverse_blocks(key, part):
    shape = (NSUBS, BLOCKS, BLOCK, BLOCK)
    noise = jax.random.normal(key, shape, jnp.float32)
    return jnp.eye(BLOCK, dtype=jnp.float32) + noise * (0.35 / math.sqrt(BLOCK))


def level_of(stream_key, extent, pieces, least, top_value):
    factor_of = 1.0
    for axis_at, shards_of in pieces:
        steps = jax.random.uniform(jax.random.fold_in(jax.random.fold_in(stream_key, 6), axis_at), (shards_of,), jnp.float32, least / len(pieces), top_value / len(pieces))
        factor_of = factor_of * jnp.repeat(jnp.exp(steps), extent[axis_at] // shards_of).reshape((-1,) + (1,) * (len(extent) - 1 - axis_at))
    return factor_of


def centred(own_key, shape, deviation, most, shards=(), kind=jnp.bfloat16):
    factor_of = level_of(own_key, shape, shards, -0.22, 0.18) if shards else 1.0
    drawn = jax.random.normal(own_key, shape, jnp.float32) * deviation * factor_of
    return jnp.minimum(jnp.maximum(drawn, -most), most).astype(kind)


def setup_inputs(seed: int = 0) -> dict:
    keys = jax.random.split(jax.random.key(seed), 6)
    return {
        "schur": draw_schur(jax.random.fold_in(keys[5], 71), 0),
        "inverse_blocks": draw_inverse_blocks(jax.random.fold_in(keys[5], 71), 0),
        "loads": centred(keys[2], (NSUBS, CASES, ORDER), 1.0, 6.0, ((0, 4), (2, 8)), jnp.float32),
        "share_list": draw_share_list(jax.random.fold_in(keys[5], 71), 0),
        "multiplicity": draw_multiplicity(jax.random.fold_in(keys[5], 71), 0),
    }


FULL_PRECISION = lax.Precision.HIGHEST

def assemble(values, share_list):
    blocks = values.reshape(NSUBS, values.shape[1], BLOCKS, BLOCK)
    selector = (share_list[..., None] == jnp.arange(BLOCKS, dtype=jnp.int32)).astype(jnp.float32)
    outgoing = jnp.einsum('ijsk,ipkd->ijspd', selector, blocks, precision=FULL_PRECISION)
    incoming = jnp.transpose(outgoing, (1, 0, 2, 3, 4))
    summed = blocks + jnp.einsum('ijsk,ijspd->ipkd', selector, incoming, precision=FULL_PRECISION)
    return summed.reshape(values.shape)

def products(left, right, row_weight):
    weighting = 1.0 / (ORDER * NSUBS)
    return jnp.einsum('ipr,iqr->pq', left * row_weight[:, None, :], right, precision=FULL_PRECISION) * weighting

def precondition(basis, inverse_blocks, block_weight, share_list):
    blocks = basis.reshape(NSUBS, CASES, BLOCKS, BLOCK)
    local = jnp.einsum('ikde,ipke->ipkd', inverse_blocks, blocks, precision=FULL_PRECISION)
    local = local * block_weight[:, None, :, None]
    return assemble(local.reshape(NSUBS, CASES, ORDER), share_list)

def apply_schur(field, schur):
    rounded = field.astype(jnp.bfloat16)

    def single(pair):
        return lax.dot_general(pair[0].astype(jnp.float32), pair[1].astype(jnp.float32), (((1,), (1,)), ((), ())), preferred_element_type=jnp.float32)
    return lax.map(single, (rounded, schur))

def lower_solve(lower, values):
    flat = jnp.transpose(values, (1, 0, 2)).reshape(CASES, -1)
    solved = jax.scipy.linalg.solve_triangular(lower, flat, lower=True)
    return jnp.transpose(solved.reshape(CASES, NSUBS, ORDER), (1, 0, 2))

def reference(schur, inverse_blocks, loads, share_list, multiplicity):
    block_weight = 1.0 / multiplicity.astype(jnp.float32)
    row_weight = jnp.repeat(block_weight, BLOCK, axis=1)
    right_side = assemble(loads, share_list)
    first = jnp.linalg.cholesky(products(right_side, right_side, row_weight))
    basis = [lower_solve(first, right_side)]
    hessen = jnp.zeros((ITERS * CASES, (ITERS + 1) * CASES), jnp.float32)
    for level in range(ITERS):
        image = assemble(apply_schur(precondition(basis[level], inverse_blocks, block_weight, share_list), schur), share_list)
        stacked = jnp.stack(basis)
        weighting = 1.0 / (ORDER * NSUBS)
        coefs = jnp.einsum('ipr,liqr->lpq', image * row_weight[:, None, :], stacked, precision=FULL_PRECISION) * weighting
        image = image - jnp.einsum('lpq,liqr->ipr', coefs, stacked, precision=FULL_PRECISION)
        lower = jnp.linalg.cholesky(products(image, image, row_weight))
        basis.append(lower_solve(lower, image))
        rows = slice(level * CASES, (level + 1) * CASES)
        for earlier in range(level + 1):
            hessen = hessen.at[rows, earlier * CASES:(earlier + 1) * CASES].set(coefs[earlier])
        hessen = hessen.at[rows, (level + 1) * CASES:(level + 2) * CASES].set(lower)
    target = jnp.zeros((CASES, (ITERS + 1) * CASES), jnp.float32).at[:, :CASES].set(first)
    normal_matrix = jnp.dot(hessen, hessen.T, precision=FULL_PRECISION)
    right_part = jnp.dot(target, hessen.T, precision=FULL_PRECISION)
    factor = jnp.linalg.cholesky(normal_matrix)
    middle = jax.scipy.linalg.solve_triangular(factor, right_part.T, lower=True)
    coeff_t = jax.scipy.linalg.solve_triangular(factor, middle, lower=True, trans=1)
    combine = coeff_t.T
    misfit = target - jnp.dot(combine, hessen, precision=FULL_PRECISION)
    update = jnp.zeros((NSUBS, CASES, ORDER), jnp.float32)
    for level in range(ITERS):
        update = update + jnp.einsum('pq,iqr->ipr', combine[:, level * CASES:(level + 1) * CASES], basis[level], precision=FULL_PRECISION)
    solution = precondition(update, inverse_blocks, block_weight, share_list)
    return (solution, misfit)
```

```python
import functools

import jax
import jax.numpy as jnp
from jax import lax
from jax.experimental import pallas as pl
from jax.experimental.pallas import tpu as pltpu
from jax.sharding import PartitionSpec as P

F32 = jnp.float32
BF16 = jnp.bfloat16
HIGH = lax.Precision.HIGHEST
VM = pl.BlockSpec(memory_space=pltpu.VMEM)
SM = pl.BlockSpec(memory_space=pltpu.SMEM)


def nn(a, b):
    return lax.dot_general(a, b, (((1,), (0,)), ((), ())), precision=HIGH, preferred_element_type=F32)


def nt(a, b):
    return lax.dot_general(a, b, (((1,), (1,)), ((), ())), precision=HIGH, preferred_element_type=F32)


def nt16(a, b):
    return lax.dot_general(a, b, (((1,), (1,)), ((), ())), preferred_element_type=F32)


def pair_sum(values):
    while len(values) > 1:
        values = [values[i] + values[i + 1] for i in range(0, len(values), 2)]
    return values[0]


def factor(mats):
    size = mats[0].shape[0]
    rows = lax.broadcasted_iota(jnp.int32, (size, size), 0)
    cols = lax.broadcasted_iota(jnp.int32, (size, size), 1)
    eye = (rows == cols).astype(F32)
    work = [jnp.concatenate([m, eye], axis=1) for m in mats]
    kept = [[] for _ in mats]
    for j in range(size):
        for n in range(len(mats)):
            m = work[n]
            row = m[j : j + 1, :] * lax.rsqrt(m[j : j + 1, j : j + 1])
            col = m[:, j : j + 1] * lax.rsqrt(m[j : j + 1, j : j + 1])
            kept[n].append(row)
            work[n] = m - col * row
    out = []
    for n in range(len(mats)):
        full = jnp.concatenate(kept[n], axis=0)
        out.append((jnp.where(cols >= rows, full[:, :size], 0.0), full[:, size:]))
    return out


def call(kernel, outs, args, specs, scratch=(), vmem=16, name=None):
    return pl.pallas_call(
        kernel,
        out_shape=outs,
        in_specs=specs,
        out_specs=jax.tree.map(lambda _: VM, outs),
        scratch_shapes=list(scratch),
        compiler_params=pltpu.CompilerParams(vmem_limit_bytes=vmem << 20),
        name=name,
    )(*args)


def xor(size, m):
    return [(i, i ^ m) for i in range(size)]


def body(schur, inverse_blocks, loads, share_list, multiplicity):
    matrix = schur[0]
    inverse = inverse_blocks[0]
    local_rows, order = matrix.shape
    owned, block = inverse.shape[0], inverse.shape[-1]
    cases = loads.shape[1]
    share = share_list[0]
    subs, slots = share.shape
    parts = lax.axis_size("blk")
    weighting = 1.0 / (order * subs)
    weight = 1.0 / multiplicity[0].astype(F32)
    peers = list(range(1, subs))
    cube = (owned, cases, block)

    def sds(shape, dtype=F32):
        return jax.ShapeDtypeStruct(shape, dtype)

    def permute(v, axis, m):
        return lax.ppermute(v, axis, xor(lax.axis_size(axis), m))

    def gather(v):
        same = [v] + [permute(v, "blk", 2 * m) for m in range(1, parts // 2)]
        both = []
        for piece in same:
            both += [piece, permute(piece, "blk", 1)]
        return jnp.concatenate(both, axis=0)

    def sum_blk(v):
        total = pair_sum([v] + [permute(v, "blk", 2 * m) for m in range(1, parts // 2)])
        return total + permute(total, "blk", 1)

    def to_subs(vs):
        return [permute(v, "sub", m) for m, v in zip(peers, vs)]

    def place(k, me):
        return ((k // owned) ^ me) * owned + k % owned

    def select(pieces):
        dtype = pieces.dtype

        def kernel(share_ref, p_ref, *outs):
            me, mine = lax.axis_index("blk"), lax.axis_index("sub")
            for m, o in zip(peers, outs):
                for s in range(slots):
                    k = share_ref[mine ^ m, s]
                    value = p_ref[place(jnp.maximum(k, 0), me)]
                    o[s] = jnp.where(k >= 0, value, jnp.zeros_like(value))

        outs = tuple(sds((slots, cases, block), dtype) for _ in peers)
        return call(kernel, outs, (share, pieces), [SM, VM], name="select")

    def select_all(pieces):
        dtype = pieces.dtype

        def kernel(share_ref, p_ref, o_ref):
            me = lax.axis_index("blk")
            for j in range(subs):
                for s in range(slots):
                    k = share_ref[j, s]
                    value = p_ref[place(jnp.maximum(k, 0), me)]
                    o_ref[j * slots + s] = jnp.where(k >= 0, value, jnp.zeros_like(value))

        return call(kernel, sds((subs * slots, cases, block), dtype), (share, pieces), [SM, VM], name="select_all")

    def add_shared(share_ref, acc_ref, arrived):
        me, mine = lax.axis_index("blk"), lax.axis_index("sub")
        for m, a_ref in zip(peers, arrived):
            for s in range(slots):
                k = share_ref[mine ^ m, s]

                @pl.when(jnp.logical_and(k >= 0, k // owned == me))
                def _():
                    acc_ref[k % owned] += a_ref[s].astype(F32)

    n_in = len(peers)

    def begin(raw):
        def kernel(l_ref, b_ref, g_ref):
            value = l_ref[...]
            for k in range(owned):
                b_ref[k] = value[:, k * block : (k + 1) * block]
            g_ref[...] = nt(value, value) * weighting

        return call(kernel, (sds(cube), sds((cases, cases))), (raw,), [VM], name="begin")

    def start(own, arrived, grams):
        def kernel(share_ref, w_ref, own_ref, inv_ref, g_ref, *rest):
            ins, outs = rest[:n_in], rest[n_in:]
            b_ref, x_ref, h_ref, f_ref = outs
            ((up, inv_low),) = factor([g_ref[...]])
            f_ref[...] = up
            b_ref[...] = own_ref[...]
            add_shared(share_ref, b_ref, ins)
            for k in range(owned):
                value = nn(inv_low, b_ref[k])
                b_ref[k] = value
                value = nt(value, inv_ref[k]) * w_ref[k]
                x_ref[k] = value
                h_ref[k] = value.astype(BF16)

        outs = (sds(cube), sds(cube), sds(cube, BF16), sds((cases, cases)))
        return call(kernel, outs, (share, weight, own, inverse, grams, *arrived), [SM, SM] + [VM] * (3 + n_in), name="start")

    def middle(own, arrived):
        def kernel(share_ref, w_ref, own_ref, inv_ref, *rest):
            ins, outs = rest[:n_in], rest[n_in:]
            k_ref, x_ref, h_ref = outs
            k_ref[...] = own_ref[...]
            add_shared(share_ref, k_ref, ins)
            for k in range(owned):
                value = nt(k_ref[k], inv_ref[k]) * w_ref[k]
                x_ref[k] = value
                h_ref[k] = value.astype(BF16)

        outs = (sds(cube), sds(cube), sds(cube, BF16))
        return call(kernel, outs, (share, weight, own, inverse, *arrived), [SM, SM] + [VM] * (2 + n_in), name="middle")

    def multiply(pieces):
        def kernel(m_ref, p_ref, y_ref):
            me = lax.axis_index("blk")
            total = jnp.zeros((cases, local_rows), F32)
            for q in range(parts):
                z = jnp.concatenate([p_ref[q * owned + i] for i in range(owned)], axis=1)
                at = pl.multiple_of((q ^ me) * local_rows, local_rows)
                total = total + nt16(z, m_ref[:, pl.ds(at, local_rows)])
            y_ref[...] = total

        return call(kernel, sds((cases, local_rows)), (matrix, pieces), [VM, VM], vmem=6, name="multiply")

    def multiply_shared(part, arrived):
        def kernel(share_ref, m_ref, part_ref, *rest):
            ins, (y_ref, h_ref) = rest[:n_in], rest[n_in:]
            mine = lax.axis_index("sub")
            total = part_ref[...]
            for m, a_ref in zip(peers, ins):
                z = jnp.concatenate([a_ref[s] for s in range(slots)], axis=1)
                cols = []
                for s in range(slots):
                    at = pl.multiple_of(jnp.maximum(share_ref[mine ^ m, s], 0) * block, block)
                    cols.append(m_ref[:, pl.ds(at, block)])
                total = total + nt16(z, jnp.concatenate(cols, axis=1))
            for k in range(owned):
                value = total[:, k * block : (k + 1) * block]
                y_ref[k] = value
                h_ref[k] = value.astype(BF16)

        outs = (sds(cube), sds(cube, BF16))
        return call(
            kernel, outs, (share, matrix, part, *arrived), [SM] + [VM] * (2 + n_in), vmem=6, name="multiply_shared"
        )

    def apply(half):
        pieces = gather(half)
        arrived = to_subs(select(pieces))
        image, image_half = multiply_shared(multiply(pieces), arrived)
        return arrived, image, image_half

    def inner(b, k1, y1):
        def kernel(w_ref, b_ref, k_ref, y_ref, g_ref):
            wide = lambda ref: jnp.concatenate([ref[k] for k in range(owned)], axis=1)
            weighted = lambda ref: jnp.concatenate([ref[k] * w_ref[k] for k in range(owned)], axis=1)
            bb, kk, yy = wide(b_ref), wide(k_ref), wide(y_ref)
            left = jnp.concatenate([weighted(b_ref), weighted(k_ref), yy], axis=0)
            right = jnp.concatenate([bb, kk, yy], axis=0)
            g_ref[...] = nt(left, right) * weighting

        return call(kernel, sds((3 * cases, 3 * cases)), (weight, b, k1, y1), [SM] + [VM] * 3, name="inner")

    def finish(gram, mine_slots, their_slots, upper, x0, in0, x1, in1):
        def kernel(share_ref, g_ref, s_ref, f_ref, x0_ref, x1_ref, *rest):
            theirs, in0_refs, in1_refs = rest[:n_in], rest[n_in : 2 * n_in], rest[2 * n_in : 3 * n_in]
            sol_ref, mis_ref, all_ref, z0_ref, z1_ref = rest[3 * n_in :]
            mine = lax.axis_index("sub")
            z0_ref[...] = x0_ref[...]
            add_shared(share_ref, z0_ref, in0_refs)
            z1_ref[...] = x1_ref[...]
            add_shared(share_ref, z1_ref, in1_refs)
            all_ref[mine] = s_ref[...]
            for m, t_ref in zip(peers, theirs):
                all_ref[mine ^ m] = t_ref[...]
            cross = jnp.zeros((cases, cases), F32)
            for i in range(subs):
                for j in range(i + 1, subs):
                    left = jnp.concatenate([all_ref[i, j * slots + s] for s in range(slots)], axis=1)
                    right = jnp.concatenate([all_ref[j, i * slots + s] for s in range(slots)], axis=1)
                    cross = cross + nt16(left, right) + nt16(right, left)
            n = cases
            g = lambda r, c: g_ref[r * n : (r + 1) * n, c * n : (c + 1) * n]
            g00, g10, g11, g20, g21 = g(0, 0), g(1, 0), g(1, 1), g(2, 0), g(2, 1)
            g22 = g(2, 2) + cross * weighting
            (u00, i00), (_, j1) = factor([g00, g11])
            l10 = nt(g10, i00)
            l20 = nt(g20, i00)
            k21 = nt(g21, j1)
            ((u11, i11),) = factor([g11 - nt(l10, l10)])
            l21 = nt(g21 - nt(l20, l10), i11)
            (u22, _), (_, j2) = factor([g22 - nt(l20, l20) - nt(l21, l21), g22 - nt(k21, k21)])
            tn = lambda a, b: lax.dot_general(a, b, (((0,), (1,)), ((), ())), precision=HIGH, preferred_element_type=F32)
            r1 = tn(g10, j1)
            r2 = nt(tn(g20, jnp.eye(n, dtype=F32)) - nt(r1, k21), j2)
            c1 = nn(r2, j2)
            c0 = nn(r1 - nn(c1, k21), j1)
            up = f_ref[...]
            down = lambda v: lax.dot_general(up, v, (((0,), (0,)), ((), ())), precision=HIGH, preferred_element_type=F32)
            tt = lambda u: u.T
            m0 = tt(u00) - nn(c0, l10) - nn(c1, l20)
            m1 = -nt(c0, u11) - nn(c1, l21)
            m2 = -nt(c1, u22)
            mis_ref[...] = down(jnp.concatenate([m0, m1, m2], axis=1))
            c0, c1 = down(c0), down(c1)
            for k in range(owned):
                sol_ref[:, k * block : (k + 1) * block] = nn(c0, z0_ref[k]) + nn(c1, z1_ref[k])

        outs = (sds((cases, local_rows)), sds((cases, 3 * cases)))
        return call(
            kernel,
            outs,
            (share, gram, mine_slots, upper, x0, x1, *their_slots, *in0, *in1),
            [SM] + [VM] * (5 + 3 * n_in),
            scratch=[pltpu.VMEM((subs, subs * slots, cases, block), BF16), pltpu.VMEM(cube, F32), pltpu.VMEM(cube, F32)],
            name="finish",
        )

    own, gram0 = begin(loads[0])
    gram0 = sum_blk(gram0)
    gram0 = pair_sum([gram0] + [permute(gram0, "sub", m) for m in peers])
    b, x0, half, upper = start(own, to_subs(select(gather(own))), gram0)
    in0, y0, half = apply(half)
    k1, x1, half = middle(y0, to_subs(select(gather(half))))
    in1, y1, half = apply(half)
    gram = sum_blk(inner(b, k1, y1))
    gram = pair_sum([gram] + [permute(gram, "sub", m) for m in peers])
    mine_slots = select_all(gather(half))
    solution, misfit = finish(
        gram, mine_slots, to_subs([mine_slots] * n_in), upper, x0, in0, x1, in1
    )
    return (solution[None], misfit)


def solution(mesh):
    placed = (
        P("sub", "blk", None),
        P("sub", "blk", None, None),
        P("sub", None, "blk"),
        P("sub", None, None),
        P("sub", "blk"),
    )
    return jax.shard_map(
        body, mesh=mesh, in_specs=placed, out_specs=(P("sub", None, "blk"), P()), check_vma=False
    )
```

```python
import functools

import jax
import jax.numpy as jnp
from jax import lax
from jax.experimental import pallas as pl
from jax.experimental.pallas import tpu as pltpu
from jax.sharding import PartitionSpec as P

F32 = jnp.float32
BF16 = jnp.bfloat16
HIGH = lax.Precision.HIGHEST
VM = pl.BlockSpec(memory_space=pltpu.VMEM)
SM = pl.BlockSpec(memory_space=pltpu.SMEM)


def nn(a, b):
    return lax.dot_general(a, b, (((1,), (0,)), ((), ())), precision=HIGH, preferred_element_type=F32)


def nt(a, b):
    return lax.dot_general(a, b, (((1,), (1,)), ((), ())), precision=HIGH, preferred_element_type=F32)


def nt16(a, b):
    return lax.dot_general(a, b, (((1,), (1,)), ((), ())), preferred_element_type=F32)


def pair_sum(values):
    while len(values) > 1:
        values = [values[i] + values[i + 1] for i in range(0, len(values), 2)]
    return values[0]


def factor(mats):
    size = mats[0].shape[0]
    rows = lax.broadcasted_iota(jnp.int32, (size, size), 0)
    cols = lax.broadcasted_iota(jnp.int32, (size, size), 1)
    eye = (rows == cols).astype(F32)
    work = [jnp.concatenate([m, eye], axis=1) for m in mats]
    kept = [[] for _ in mats]
    for j in range(size):
        for n in range(len(mats)):
            m = work[n]
            row = m[j : j + 1, :] * lax.rsqrt(m[j : j + 1, j : j + 1])
            col = m[:, j : j + 1] * lax.rsqrt(m[j : j + 1, j : j + 1])
            kept[n].append(row)
            work[n] = m - col * row
    out = []
    for n in range(len(mats)):
        full = jnp.concatenate(kept[n], axis=0)
        out.append((jnp.where(cols >= rows, full[:, :size], 0.0), full[:, size:]))
    return out


def cut3(v):
    high = v.astype(BF16)
    rest = v - high.astype(F32)
    mid = rest.astype(BF16)
    return high, mid, (rest - mid.astype(F32)).astype(BF16)


def join3(parts):
    high, mid, low = (p.astype(F32) for p in parts)
    return high + (mid + low)


def call(kernel, outs, args, specs, scratch=(), vmem=8, name=None, cost=None):
    return pl.pallas_call(
        kernel,
        out_shape=outs,
        in_specs=specs,
        out_specs=jax.tree.map(lambda _: VM, outs),
        scratch_shapes=list(scratch),
        compiler_params=pltpu.CompilerParams(vmem_limit_bytes=vmem << 20),
        cost_estimate=cost,
        name=name,
    )(*args)


def xor(size, m):
    return [(i, i ^ m) for i in range(size)]


EXTRA = 3


def body(schur, inverse_blocks, loads, share_list, multiplicity):
    inverse = inverse_blocks[0]
    local_rows, order = schur.shape[1:]
    owned, block = inverse.shape[0], inverse.shape[-1]
    cases = loads.shape[1]
    share = share_list[0]
    subs, slots = share.shape
    parts = lax.axis_size("blk")
    weighting = 1.0 / (order * subs)
    weight = 1.0 / multiplicity[0].astype(F32)
    peers = list(range(1, subs))
    n_in = len(peers)
    cube = (owned, cases, block)
    pad = block - 3 * cases

    def sds(shape, dtype=F32):
        return jax.ShapeDtypeStruct(shape, dtype)

    def permute(v, axis, m):
        return lax.ppermute(v, axis, xor(lax.axis_size(axis), m))

    def to_subs(vs):
        return [permute(v, "sub", m) for m, v in zip(peers, vs)]

    def padded(v):
        return jnp.concatenate([v, jnp.zeros((cases, block - v.shape[1]), v.dtype)], axis=1)

    def me_blk():
        return lax.axis_index("blk")

    def me_sub():
        return lax.axis_index("sub")


    def masked(share_ref, own, dtype, outs):
        for m, o_ref in zip(peers, outs):
            for s in range(slots):
                k = share_ref[me_sub() ^ m, s]
                here = jnp.logical_and(k >= 0, k // owned == me_blk())
                value = own(jnp.where(here, k % owned, 0))
                o_ref[s] = jnp.where(here, value, jnp.zeros_like(value)).astype(dtype)

    def route(outs, extra=None):
        arrived = to_subs(outs)
        dtype = arrived[0].dtype
        total = n_in * slots + (extra is not None)
        half = (total + 1) // 2

        def kernel(*refs):
            ins, (keep_ref, send_ref, all_ref) = refs[:-3], refs[-3:]
            side = me_blk() % 2
            for i in range(2 * half):
                at = all_ref.at[i // half, i % half]
                if i < n_in * slots:
                    at[...] = ins[i // slots][i % slots]
                elif i < total:
                    at[...] = pair_sum([ins[-1][...]] + [r[slots] for r in ins[:n_in]])
                else:
                    at[...] = jnp.zeros((cases, block), dtype)
            keep_ref[...] = all_ref[side]
            send_ref[...] = all_ref[1 - side]

        args = tuple(arrived) + (() if extra is None else (extra,))
        shape = (half, cases, block)
        keep, send = call(
            kernel,
            (sds(shape, dtype), sds(shape, dtype)),
            args,
            [VM] * len(args),
            scratch=[pltpu.VMEM((2,) + shape, dtype)],
            name="split",
        )
        keep = keep + permute(send, "blk", 1)
        far = [permute(keep, "blk", 2 * m) for m in reversed(range(1, parts // 2))]
        keep = pair_sum([keep] + far[::-1])
        return keep, permute(keep, "blk", 1)

    def routed(refs, all_ref):
        side = me_blk() % 2
        all_ref[side] = refs[0][...]
        all_ref[1 - side] = refs[1][...]
        half = all_ref.shape[1]
        return lambda i: all_ref[i // half, i % half]

    def add_shared(share_ref, acc_ref, arrived):
        for n, m in enumerate(peers):
            for s in range(slots):
                k = share_ref[me_sub() ^ m, s]

                @pl.when(jnp.logical_and(k >= 0, k // owned == me_blk()))
                def _():
                    acc_ref[k % owned] += arrived(n, s).astype(F32)


    def gather(v):
        far = {m: permute(v, "blk", 2 * m) for m in reversed(range(1, parts // 2))}
        far[0] = v
        both = []
        for m in range(parts // 2):
            both += [far[m], permute(far[m], "blk", 1)]
        near = max(2, parts // 2)
        rest = both[near:]
        return [jnp.concatenate(both[:near], axis=0)] + ([jnp.concatenate(rest, axis=0)] if rest else [])

    def piece_reader(p_refs, stride):
        sizes = [r.shape[0] // stride for r in p_refs]

        def read(k):
            q, r = (k // owned) ^ me_blk(), k % owned
            value = p_refs[0][jnp.minimum(q, sizes[0] - 1) * stride + r]
            if len(p_refs) > 1:
                other = p_refs[1][jnp.maximum(q - sizes[0], 0) * stride + r]
                value = jnp.where(q < sizes[0], value, other)
            return value

        return read

    def extra_sum(p_refs, stride):
        found = []
        for r in p_refs:
            for q in range(r.shape[0] // stride):
                found.append(join3([r[q * stride + owned + e] for e in range(EXTRA)]))
        return pair_sum(found)

    def select(pieces, extra, joined):
        stride = owned + (EXTRA if extra else 0)
        n_p = len(pieces)
        more = EXTRA if extra else 0

        def kernel(share_ref, *refs):
            p_refs, outs = refs[:n_p], refs[n_p:]
            read = piece_reader(p_refs, stride)
            for n, m in enumerate(peers):
                for s in range(slots):
                    k = share_ref[me_sub() ^ m, s]
                    value = read(jnp.maximum(k, 0))
                    value = jnp.where(k >= 0, value, jnp.zeros_like(value))
                    if joined:
                        outs[0][n * slots + s] = value
                    else:
                        outs[n][s] = value
            if extra:
                total = extra_sum(p_refs, stride)
                outs[-1][...] = total
                for e, part in enumerate(cut3(total)):
                    for o in outs[:-1]:
                        o[o.shape[0] - EXTRA + e] = part

        if joined:
            outs = [sds((n_in * slots + more, cases, block), BF16)]
        else:
            outs = [sds((slots + more, cases, block), BF16) for _ in peers]
        if extra:
            outs.append(sds((cases, block)))
        return call(kernel, tuple(outs), (share, *pieces), [SM] + [VM] * n_p, name="select")


    def open_(raw):
        def kernel(share_ref, l_ref, b_ref, g_ref, *outs):
            value = l_ref[...]
            for k in range(owned):
                b_ref[k] = value[:, k * block : (k + 1) * block]
            gram = padded(nt(value, value) * weighting)
            g_ref[...] = gram
            masked(share_ref, lambda k: b_ref[k], F32, outs)
            for o_ref in outs:
                o_ref[slots] = gram

        outs = (sds(cube), sds((cases, block))) + tuple(sds((slots + 1, cases, block)) for _ in peers)
        return call(kernel, outs, (share, raw), [SM, VM], name="open")

    def fetch(full, after):
        def kernel(m_ref, a_ref, o_ref, sem):
            copy = pltpu.make_async_copy(m_ref, o_ref, sem)
            copy.start()
            copy.wait()

        anywhere = pl.BlockSpec(memory_space=pl.ANY)
        cost = pl.CostEstimate(flops=0, transcendentals=0, bytes_accessed=2 * full.size * 2)
        return call(
            kernel,
            sds(full.shape, full.dtype),
            (full, after),
            [anywhere, anywhere],
            scratch=[pltpu.SemaphoreType.DMA],
            name="fetch",
            cost=cost,
        )

    def start(own, arrived):
        half = arrived[0].shape[0]

        def kernel(share_ref, w_ref, own_ref, inv_ref, a0, a1, b_ref, x_ref, h_ref, f_ref, all_ref):
            at = routed((a0, a1), all_ref)
            ((up, inv_low),) = factor([at(n_in * slots)[:, :cases]])
            f_ref[...] = up
            b_ref[...] = own_ref[...]
            add_shared(share_ref, b_ref, lambda n, s: at(n * slots + s))
            for k in range(owned):
                value = nn(inv_low, b_ref[k])
                b_ref[k] = value
                value = nt(value, inv_ref[k]) * w_ref[k]
                x_ref[k] = value
                h_ref[k] = value.astype(BF16)

        outs = (sds(cube), sds(cube), sds(cube, BF16), sds((cases, cases)))
        return call(
            kernel,
            outs,
            (share, weight, own, inverse, *arrived),
            [SM, SM] + [VM] * 4,
            scratch=[pltpu.VMEM((2, half, cases, block), F32)],
            name="start",
        )

    def middle(own, base, arrived):
        half = arrived[0].shape[0]

        def kernel(share_ref, w_ref, own_ref, base_ref, inv_ref, a0, a1, x_ref, h_ref, k_ref, all_ref):
            at = routed((a0, a1), all_ref)
            k_ref[...] = own_ref[...]
            add_shared(share_ref, k_ref, lambda n, s: at(n * slots + s))
            for k in range(owned):
                value = nt(k_ref[k], inv_ref[k]) * w_ref[k]
                x_ref[k] = value
                h_ref[k] = value.astype(BF16)
            wide = lambda ref: jnp.concatenate([ref[k] for k in range(owned)], axis=1)
            weighted = lambda ref: jnp.concatenate([ref[k] * w_ref[k] for k in range(owned)], axis=1)
            g0 = nt(weighted(base_ref), wide(base_ref))
            g1 = nt(weighted(k_ref), jnp.concatenate([wide(base_ref), wide(k_ref)], axis=0))
            gram = padded(jnp.concatenate([g0, g1], axis=1) * weighting)
            for e, part in enumerate(cut3(gram)):
                h_ref[owned + e] = part

        outs = (sds(cube), sds((owned + EXTRA, cases, block), BF16), sds(cube))
        return call(
            kernel,
            outs,
            (share, weight, own, base, inverse, *arrived),
            [SM, SM] + [VM] * 5,
            scratch=[pltpu.VMEM((2, half, cases, block), BF16)],
            name="middle",
        )

    def multiply(matrix, pieces, first, stride, before):
        count = pieces.shape[0] // stride

        def kernel(m_ref, p_ref, *rest):
            y_ref = rest[-1]
            total = rest[0][...] if len(rest) > 1 else jnp.zeros((cases, local_rows), F32)
            for q in range(count):
                z = jnp.concatenate([p_ref[q * stride + i] for i in range(owned)], axis=1)
                at = pl.multiple_of(((first + q) ^ me_blk()) * local_rows, local_rows)
                total = total + nt16(z, m_ref[:, pl.ds(at, local_rows)])
            y_ref[...] = total

        args = (matrix, pieces) + (() if before is None else (before,))
        cost = pl.CostEstimate(
            flops=2 * cases * local_rows * local_rows * count, transcendentals=0, bytes_accessed=2 * local_rows * local_rows * count
        )
        return call(kernel, sds((cases, local_rows)), args, [VM] * len(args), name="multiply", cost=cost)

    def shared_product(share_ref, m_ref, total, ins):
        for m, a_ref in zip(peers, ins):
            z = jnp.concatenate([a_ref[s] for s in range(slots)], axis=1)
            cols = []
            for s in range(slots):
                at = pl.multiple_of(jnp.maximum(share_ref[me_sub() ^ m, s], 0) * block, block)
                cols.append(m_ref[:, pl.ds(at, block)])
            total = total + nt16(z, jnp.concatenate(cols, axis=1))
        return total

    def tail_route(matrix, part, arrived):
        def kernel(share_ref, m_ref, part_ref, *rest):
            ins, y_ref, outs = rest[:n_in], rest[n_in], rest[n_in + 1 :]
            total = shared_product(share_ref, m_ref, part_ref[...], ins)
            for k in range(owned):
                y_ref[k] = total[:, k * block : (k + 1) * block]
            masked(share_ref, lambda k: y_ref[k], BF16, outs)

        outs = (sds(cube),) + tuple(sds((slots, cases, block), BF16) for _ in peers)
        return call(kernel, outs, (share, matrix, part, *arrived), [SM] + [VM] * (2 + n_in), name="tail_route")

    def tail_gram(matrix, part, arrived, b, k1):
        def kernel(share_ref, m_ref, part_ref, b_ref, k_ref, *rest):
            ins, h_ref = rest[:n_in], rest[n_in]
            total = shared_product(share_ref, m_ref, part_ref[...], ins)
            for k in range(owned):
                h_ref[k] = total[:, k * block : (k + 1) * block].astype(BF16)
            wide = lambda ref: jnp.concatenate([ref[k] for k in range(owned)], axis=1)
            gram = nt(total, jnp.concatenate([wide(b_ref), wide(k_ref), total], axis=0))
            for e, part in enumerate(cut3(padded(gram * weighting))):
                h_ref[owned + e] = part

        outs = sds((owned + EXTRA, cases, block), BF16)
        return call(
            kernel, outs, (share, matrix, part, b, k1, *arrived), [SM] + [VM] * (4 + n_in), name="tail_gram"
        )

    def gram_of(g_ref, ins):
        return pair_sum([g_ref[...]] + [join3([r[r.shape[0] - EXTRA + e] for e in range(EXTRA)]) for r in ins])

    n = cases

    def early(g01, arrived):
        def kernel(g_ref, *rest):
            ins, (u00_ref, i00_ref, l10_ref, u11_ref, i11_ref, j1_ref, r1_ref) = rest[:n_in], rest[n_in:]
            g = gram_of(g_ref, ins)
            g00, g10, g11 = g[:, :n], g[:, n : 2 * n], g[:, 2 * n : 3 * n]
            (u00, i00), (_, j1) = factor([g00, g11])
            l10 = nt(g10, i00)
            ((u11, i11),) = factor([g11 - nt(l10, l10)])
            u00_ref[...] = u00
            i00_ref[...] = i00
            l10_ref[...] = l10
            u11_ref[...] = u11
            i11_ref[...] = i11
            j1_ref[...] = j1
            r1_ref[...] = nt(g10.T, j1)

        outs = tuple(sds((n, n)) for _ in range(7))
        cost = pl.CostEstimate(flops=10**8, transcendentals=0, bytes_accessed=10**7)
        return call(kernel, outs, (g01, *arrived), [VM] * (1 + n_in), name="early", cost=cost)

    def finish(g2, mine_slots, their_slots, known, upper, x0, in0, x1, in1):
        n_known = len(known)

        def kernel(share_ref, g_ref, s_ref, f_ref, x0_ref, x1_ref, *rest):
            known_refs, rest = rest[:n_known], rest[n_known:]
            theirs, in0_refs, in1_refs = rest[:n_in], rest[n_in : 2 * n_in], rest[2 * n_in : 3 * n_in]
            sol_ref, mis_ref, all_ref, z0_ref, z1_ref = rest[3 * n_in :]
            u00, i00, l10, u11, i11, j1, r1 = (r[...] for r in known_refs)
            z0_ref[...] = x0_ref[...]
            add_shared(share_ref, z0_ref, lambda p, s: in0_refs[p][s])
            z1_ref[...] = x1_ref[...]
            add_shared(share_ref, z1_ref, lambda p, s: in1_refs[p][s])
            all_ref[me_sub()] = s_ref[...]
            for m, t_ref in zip(peers, theirs):
                all_ref[me_sub() ^ m] = t_ref[...]
            cross = jnp.zeros((n, n), F32)
            for i in range(subs):
                for j in range(i + 1, subs):
                    at = ((i ^ j) - 1) * slots
                    left = jnp.concatenate([all_ref[i, at + s] for s in range(slots)], axis=1)
                    right = jnp.concatenate([all_ref[j, at + s] for s in range(slots)], axis=1)
                    cross = cross + nt16(left, right)
            g = gram_of(g_ref, theirs)
            g20, g21 = g[:, :n], g[:, n : 2 * n]
            g22 = g[:, 2 * n : 3 * n] + (cross + cross.T) * weighting
            l20 = nt(g20, i00)
            k21 = nt(g21, j1)
            l21 = nt(g21 - nt(l20, l10), i11)
            (u22, _), (_, j2) = factor([g22 - nt(l20, l20) - nt(l21, l21), g22 - nt(k21, k21)])
            r2 = nt(g20.T - nt(r1, k21), j2)
            c1 = nn(r2, j2)
            c0 = nn(r1 - nn(c1, k21), j1)
            low = f_ref[...].T
            m0 = u00.T - nn(c0, l10) - nn(c1, l20)
            m1 = -nt(c0, u11) - nn(c1, l21)
            m2 = -nt(c1, u22)
            mixed = nn(low, jnp.concatenate([m0, m1, m2, c0, c1], axis=1))
            mis_ref[...] = mixed[:, : 3 * n]
            both = mixed[:, 3 * n :]
            for k in range(owned):
                z = jnp.concatenate([z0_ref[k], z1_ref[k]], axis=0)
                sol_ref[:, k * block : (k + 1) * block] = nn(both, z)

        outs = (sds((n, local_rows)), sds((n, 3 * n)))
        return call(
            kernel,
            outs,
            (share, g2, mine_slots, upper, x0, x1, *known, *their_slots, *in0, *in1),
            [SM] + [VM] * (5 + n_known + 3 * n_in),
            scratch=[
                pltpu.VMEM((subs,) + mine_slots.shape, BF16),
                pltpu.VMEM(cube, F32),
                pltpu.VMEM(cube, F32),
            ],
            name="finish",
        )

    def product(matrix, half, extra):
        stride = owned + (EXTRA if extra else 0)
        pieces = gather(half)
        chosen = select(pieces, extra, False)
        arrived = to_subs(chosen[:n_in])
        part, first = None, 0
        for p in pieces:
            part = multiply(matrix, p, first, stride, part)
            first += p.shape[0] // stride
        return part, arrived, chosen[-1]

    own, gram0, *outs = open_(loads[0])
    matrix = fetch(schur[0], gram0)
    b, x0, half, upper = start(own, route(outs, gram0))
    part, in0, _ = product(matrix, half, False)
    y0, *outs = tail_route(matrix, part, in0)
    x1, half, k1 = middle(y0, b, route(outs))
    part, in1, g01 = product(matrix, half, True)
    known = early(g01, in1)
    half = tail_gram(matrix, part, in1, b, k1)
    mine_slots, g2 = select(gather(half), True, True)
    solution, misfit = finish(g2, mine_slots, to_subs([mine_slots] * n_in), known, upper, x0, in0, x1, in1)
    return (solution[None], misfit)


def solution(mesh):
    placed = (
        P("sub", "blk", None),
        P("sub", "blk", None, None),
        P("sub", None, "blk"),
        P("sub", None, None),
        P("sub", "blk"),
    )
    return jax.shard_map(
        body, mesh=mesh, in_specs=placed, out_specs=(P("sub", None, "blk"), P()), check_vma=False
    )
```

```python
import functools

import jax
import jax.numpy as jnp
from jax import lax
from jax.experimental import pallas as pl
from jax.experimental.pallas import tpu as pltpu
from jax.sharding import PartitionSpec as P

F32 = jnp.float32
BF16 = jnp.bfloat16
HIGH = lax.Precision.HIGHEST
VM = pl.BlockSpec(memory_space=pltpu.VMEM)
SM = pl.BlockSpec(memory_space=pltpu.SMEM)


def nn(a, b):
    return lax.dot_general(a, b, (((1,), (0,)), ((), ())), precision=HIGH, preferred_element_type=F32)


def nt(a, b):
    return lax.dot_general(a, b, (((1,), (1,)), ((), ())), precision=HIGH, preferred_element_type=F32)


def nt16(a, b):
    return lax.dot_general(a, b, (((1,), (1,)), ((), ())), preferred_element_type=F32)


def pair_sum(values):
    while len(values) > 1:
        values = [values[i] + values[i + 1] for i in range(0, len(values), 2)]
    return values[0]


def factor(mats):
    size = mats[0].shape[0]
    rows = lax.broadcasted_iota(jnp.int32, (size, size), 0)
    cols = lax.broadcasted_iota(jnp.int32, (size, size), 1)
    eye = (rows == cols).astype(F32)
    work = [jnp.concatenate([m, eye], axis=1) for m in mats]
    kept = [[] for _ in mats]
    for j in range(size):
        for n in range(len(mats)):
            m = work[n]
            row = m[j : j + 1, :] * lax.rsqrt(m[j : j + 1, j : j + 1])
            col = m[:, j : j + 1] * lax.rsqrt(m[j : j + 1, j : j + 1])
            kept[n].append(row)
            work[n] = m - col * row
    out = []
    for n in range(len(mats)):
        full = jnp.concatenate(kept[n], axis=0)
        out.append((jnp.where(cols >= rows, full[:, :size], 0.0), full[:, size:]))
    return out


def cut3(v):
    high = v.astype(BF16)
    rest = v - high.astype(F32)
    mid = rest.astype(BF16)
    return high, mid, (rest - mid.astype(F32)).astype(BF16)


def join3(parts):
    high, mid, low = (p.astype(F32) for p in parts)
    return high + (mid + low)


def call(kernel, outs, args, specs, scratch=(), vmem=8, name=None, cost=None):
    return pl.pallas_call(
        kernel,
        out_shape=outs,
        in_specs=specs,
        out_specs=jax.tree.map(lambda _: VM, outs),
        scratch_shapes=list(scratch),
        compiler_params=pltpu.CompilerParams(vmem_limit_bytes=vmem << 20),
        cost_estimate=cost,
        name=name,
    )(*args)


def xor(size, m):
    return [(i, i ^ m) for i in range(size)]


EXTRA = 3
CHUNKS = 1


def body(schur, inverse_blocks, loads, share_list, multiplicity):
    inverse = inverse_blocks[0]
    local_rows, order = schur.shape[1:]
    owned, block = inverse.shape[0], inverse.shape[-1]
    cases = loads.shape[1]
    share = share_list[0]
    subs, slots = share.shape
    parts = lax.axis_size("blk")
    zs = parts // 2
    weighting = 1.0 / (order * subs)
    weight = 1.0 / multiplicity[0].astype(F32)
    blocks = order // block
    plain = 1 - jnp.any(
        share.reshape(-1)[:, None] == jnp.arange(blocks, dtype=jnp.int32)[None, :], axis=0
    ).astype(jnp.int32)
    peers = list(range(1, subs))
    n_in = len(peers)
    n_slots = n_in * slots
    cube = (owned, cases, block)
    unit = (block // 2, block)
    per = -(-2 * n_slots // parts)
    n = cases

    def sds(shape, dtype=F32):
        return jax.ShapeDtypeStruct(shape, dtype)

    def permute(v, axis, m):
        return lax.ppermute(v, axis, xor(lax.axis_size(axis), m))

    def to_subs(vs):
        return [permute(v, "sub", m) for m, v in zip(peers, vs)]

    def padded(v):
        if v.shape[1] == block:
            return v
        return jnp.concatenate([v, jnp.zeros((v.shape[0], block - v.shape[1]), v.dtype)], axis=1)

    def me_blk():
        return lax.axis_index("blk")

    def me_sub():
        return lax.axis_index("sub")

    def wide(ref):
        return jnp.concatenate([ref[k] for k in range(owned)], axis=1)

    def weighted(ref, w_ref):
        return jnp.concatenate([ref[k] * w_ref[k] for k in range(owned)], axis=1)

    def far_and_self(v):
        far = {m: permute(v, "blk", 2 * m) for m in reversed(range(1, zs))}
        far[0] = v
        return [far[m] for m in range(zs)]


    def slot_inverse(after):
        def masked(share_ref, w_ref, inv_ref, m, s):
            k = share_ref[me_sub() ^ m, s]
            here = jnp.logical_and(k >= 0, k // owned == me_blk())
            at = jnp.where(here, k % owned, 0)
            return jnp.where(here, inv_ref[at] * w_ref[at], 0.0)

        def lend(share_ref, w_ref, inv_ref, after_ref, *outs):
            for m, o_ref in zip(peers, outs):
                for s in range(slots):
                    o_ref[s] = masked(share_ref, w_ref, inv_ref, m, s).astype(BF16)

        outs = tuple(sds((slots, block, block), BF16) for _ in peers)
        lent = call(lend, outs, (share, weight, inverse, after), [SM, SM, VM, pl.BlockSpec(memory_space=pl.ANY)], name="lend")
        arrived = to_subs(lent)

        def deal(share_ref, w_ref, inv_ref, *refs):
            ins, (keep_ref, send_ref, all_ref) = refs[:n_in], refs[n_in:]
            me = me_blk()
            for i in range(n_slots):
                m, s = peers[i // slots], i % slots
                value = masked(share_ref, w_ref, inv_ref, m, s) + ins[i // slots][s].astype(F32)
                for h in range(2):
                    u = 2 * i + h
                    all_ref[u // per, u % per] = value[h * unit[0] : (h + 1) * unit[0]]
            for u in range(2 * n_slots, parts * per):
                all_ref[u // per, u % per] = jnp.zeros(unit, F32)
            for q in range(zs):
                keep_ref[q] = all_ref[me ^ (2 * q)].astype(BF16)
                send_ref[q] = all_ref[me ^ (2 * q + 1)].astype(BF16)

        shape = (zs, per) + unit
        keep, send = call(
            deal,
            (sds(shape, BF16), sds(shape, BF16)),
            (share, weight, inverse, *arrived),
            [SM, SM] + [VM] * (1 + n_in),
            scratch=[pltpu.VMEM((parts, per) + unit, F32)],
            vmem=16,
            name="deal",
        )
        keep = keep + permute(send, "blk", 1)
        far = [permute(keep[m], "blk", 2 * m) for m in reversed(range(1, zs))]
        mine = pair_sum([v.astype(F32) for v in [keep[0]] + far[::-1]]).astype(BF16)
        same = jnp.stack(far_and_self(mine))
        return (same, permute(same, "blk", 1)), lent[0], keep, mine

    def slot_reader(same_ref, other_ref):
        def unit_at(u):
            q = (u // per) ^ me_blk()
            value, other = same_ref[q // 2, u % per], other_ref[q // 2, u % per]
            return jnp.where(q % 2 == 0, value, other)

        return lambda i: jnp.concatenate([unit_at(2 * i), unit_at(2 * i + 1)], axis=0)


    def gather(v, work, gate=()):
        pieces = far_and_self(v)
        near, far = pieces[:2], pieces[2:]
        near = jnp.concatenate([w for p in near for w in (p, permute(p, "blk", 1))], axis=0)
        done = work(near)
        if not far:
            return [near], done
        far, _, done = lax.optimization_barrier((far, gate, done))
        far = jnp.concatenate([w for p in far for w in (p, permute(p, "blk", 1))], axis=0)
        return [near, far], done

    def piece_reader(p_refs, stride):
        sizes = [r.shape[0] // stride for r in p_refs]

        def read(k):
            q, r = (k // owned) ^ me_blk(), k % owned
            value = p_refs[0][jnp.minimum(q, sizes[0] - 1) * stride + r]
            if len(p_refs) > 1:
                other = p_refs[1][jnp.maximum(q - sizes[0], 0) * stride + r]
                value = jnp.where(q < sizes[0], value, other)
            return value

        return read

    def extra_sum(p_refs, stride):
        found = []
        for r in p_refs:
            for q in range(r.shape[0] // stride):
                found.append(join3([r[q * stride + owned + e] for e in range(EXTRA)]))
        return pair_sum(found)

    def select_first(pieces, after):
        stride, n_p = owned + 1, len(pieces)

        def kernel(share_ref, after_ref, *refs):
            p_refs, outs = refs[:n_p], refs[n_p:]
            read = piece_reader(p_refs, stride)
            for i in range(n_slots):
                k = share_ref[me_sub() ^ peers[i // slots], i % slots]
                value = read(jnp.maximum(k, 0))
                outs[i // slots][i % slots] = jnp.where(k >= 0, value, jnp.zeros_like(value))
            total = pair_sum([r[q * stride + owned] for r in p_refs for q in range(r.shape[0] // stride)])
            for o_ref in outs:
                o_ref[slots] = total

        outs = tuple(sds((slots + 1, cases, block)) for _ in peers)
        anywhere = pl.BlockSpec(memory_space=pl.ANY)
        return call(kernel, outs, (share, after, *pieces), [SM, anywhere] + [VM] * n_p, name="select_first")

    def select(pieces, extra, after):
        stride = owned + (EXTRA if extra else 0)
        n_p = len(pieces)
        more = EXTRA if extra else 0

        def kernel(share_ref, after_ref, *refs):
            p_refs, outs = refs[:n_p], refs[n_p:]
            read = piece_reader(p_refs, stride)
            for i in range(n_slots):
                k = share_ref[me_sub() ^ peers[i // slots], i % slots]
                value = read(jnp.maximum(k, 0))
                value = jnp.where(k >= 0, value, jnp.zeros_like(value))
                if extra:
                    outs[0][i] = value
                else:
                    outs[i // slots][i % slots] = value
            if extra:
                total = extra_sum(p_refs, stride)
                outs[-1][...] = total
                for e, part in enumerate(cut3(total)):
                    outs[0][n_slots + e] = part

        if extra:
            outs = (sds((n_slots + more, cases, block), BF16), sds((cases, block)))
        else:
            outs = tuple(sds((slots, cases, block), BF16) for _ in peers)
        anywhere = pl.BlockSpec(memory_space=pl.ANY)
        return call(kernel, outs, (share, after, *pieces), [SM, anywhere] + [VM] * n_p, name="select")


    def mix(plain_ref, inv_ref, v_ref, x_ref, h_ref):
        for k in range(owned):
            value = v_ref[k]
            x = nt(value, inv_ref[k])
            x_ref[k] = x
            h_ref[k] = jnp.where(plain_ref[me_blk() * owned + k] > 0, x, value).astype(h_ref.dtype)

    def open_(raw):
        def kernel(plain_ref, l_ref, inv_ref, v_ref, x_ref, h_ref):
            value = l_ref[...]
            for k in range(owned):
                v_ref[k] = value[:, k * block : (k + 1) * block]
            mix(plain_ref, inv_ref, v_ref, x_ref, h_ref)
            h_ref[owned] = padded(nt(value, value) * weighting)

        outs = (sds(cube), sds(cube), sds((owned + 1, cases, block)))
        return call(kernel, outs, (plain, raw, inverse), [SM, VM, VM], name="open")

    def touch(full, after):
        def kernel(m_ref, a_ref, o_ref):
            o_ref[...] = m_ref[:8, :block].astype(F32)

        anywhere = pl.BlockSpec(memory_space=pl.ANY)
        return call(kernel, sds((8, block)), (full, after), [VM, anywhere], name="touch")

    def multiply(matrix, pieces, first, stride, before):
        count = pieces.shape[0] // stride
        wide_type = pieces.dtype == F32
        rows = local_rows // CHUNKS

        def kernel(plain_ref, p_ref, *rest):
            m_refs, y_ref = rest[:CHUNKS], rest[-1]
            totals = [
                rest[CHUNKS][:, c * rows : (c + 1) * rows] if before is not None else jnp.zeros((n, rows), F32)
                for c in range(CHUNKS)
            ]
            for q in range(count):
                owner = (first + q) ^ me_blk()
                z = []
                for i in range(owned):
                    value = p_ref[q * stride + i]
                    z.append(jnp.where(plain_ref[owner * owned + i] > 0, value, jnp.zeros_like(value)))
                z = jnp.concatenate(z, axis=1)
                if wide_type:
                    high = z.astype(BF16)
                    z = jnp.concatenate([high, (z - high.astype(F32)).astype(BF16)], axis=0)
                at = pl.multiple_of(owner * local_rows, local_rows)
                for c in range(CHUNKS):
                    found = nt16(z, m_refs[c][:, pl.ds(at, local_rows)])
                    totals[c] = totals[c] + (found[:n] + found[n:] if wide_type else found)
            for c in range(CHUNKS):
                y_ref[:, c * rows : (c + 1) * rows] = totals[c]

        args = (plain, pieces, *matrix) + (() if before is None else (before,))
        cost = pl.CostEstimate(
            flops=2 * n * local_rows * local_rows * count,
            transcendentals=0,
            bytes_accessed=2 * local_rows * local_rows * count,
        )
        return call(kernel, sds((n, local_rows)), args, [SM] + [VM] * (len(args) - 1), name="multiply", cost=cost)

    def shared_part(share_ref, m_refs, total, mine, theirs, inv_at, v_ref, x_ref, u_ref, z_ref):
        u_ref[...] = v_ref[...]
        z_ref[...] = x_ref[...]
        totals = [total[:, c * (local_rows // CHUNKS) : (c + 1) * (local_rows // CHUNKS)] for c in range(CHUNKS)]
        for p, m in enumerate(peers):
            zz, where_ = [], []
            for s in range(slots):
                k = share_ref[me_sub() ^ m, s]
                far = theirs(p, s)
                near = mine(p, s)
                if far.dtype == F32:
                    both = near + far
                    near = both.astype(BF16)
                    lower = (both - near.astype(F32)).astype(BF16)
                else:
                    lower = far
                both = nt16(jnp.concatenate([near, lower], axis=0), inv_at(p * slots + s))
                both = both[:n] + both[n:]
                high = both.astype(BF16)
                if far.dtype == F32:
                    high = jnp.concatenate([high, (both - high.astype(F32)).astype(BF16)], axis=0)
                zz.append(high)
                where_.append(pl.multiple_of(jnp.maximum(k, 0) * block, block))

                @pl.when(jnp.logical_and(k >= 0, k // owned == me_blk()))
                def _():
                    u_ref[k % owned] += far.astype(F32)
                    z_ref[k % owned] = both

            zz = jnp.concatenate(zz, axis=1)
            for c in range(CHUNKS):
                cols = jnp.concatenate([m_refs[c][:, pl.ds(at, block)] for at in where_], axis=1)
                found = nt16(zz, cols)
                totals[c] = totals[c] + (found[:n] + found[n:] if found.shape[0] > n else found)
        return jnp.concatenate(totals, axis=1)

    def tail_first(matrix, part, mine, theirs, slot_inv, v, x):
        def kernel(share_ref, plain_ref, w_ref, part_ref, inv_ref, s0, s1, v_ref, x_ref, *rest):
            m_refs, rest = rest[:CHUNKS], rest[CHUNKS:]
            mine_refs, their_refs, (y_ref, h_ref, x1_ref, u_ref, z_ref, f_ref, i_ref) = (
                rest[:n_in],
                rest[n_in : 2 * n_in],
                rest[2 * n_in :],
            )
            total = shared_part(
                share_ref,
                m_refs,
                part_ref[...],
                lambda p, s: mine_refs[p][s],
                lambda p, s: their_refs[p][s],
                slot_reader(s0, s1),
                v_ref,
                x_ref,
                u_ref,
                z_ref,
            )
            grams = [mine_refs[0][slots]] + [r[slots] for r in their_refs]
            ((up, inv_low),) = factor([pair_sum(grams)[:, :n]])
            f_ref[...] = up
            i_ref[...] = inv_low
            total = nn(inv_low, jnp.concatenate([total, wide(u_ref)], axis=1))
            total, base = total[:, :local_rows], total[:, local_rows:]
            for k in range(owned):
                y_ref[k] = total[:, k * block : (k + 1) * block]
                u_ref[k] = base[:, k * block : (k + 1) * block]
            mix(plain_ref, inv_ref, y_ref, x1_ref, h_ref)
            g0 = nt(weighted(u_ref, w_ref), base)
            g1 = nt(total, jnp.concatenate([base, total], axis=0))
            gram = padded(jnp.concatenate([g0, g1], axis=1) * weighting)
            for e, part in enumerate(cut3(gram)):
                h_ref[owned + e] = part

        outs = (sds(cube), sds((owned + EXTRA, cases, block), BF16)) + (sds(cube),) * 3 + (sds((n, n)),) * 2
        args = (share, plain, weight, part, inverse, *slot_inv, v, x, *matrix, *mine, *theirs)
        return call(kernel, outs, args, [SM] * 3 + [VM] * (len(args) - 3), vmem=16, name="tail_first")

    def tail_second(matrix, part, mine, theirs, slot_inv, v, x, base):
        def kernel(share_ref, part_ref, b_ref, s0, s1, v_ref, x_ref, mine_ref, *rest):
            m_refs, rest = rest[:CHUNKS], rest[CHUNKS:]
            their_refs, (h_ref, z_ref, u_ref) = rest[:n_in], rest[n_in:]
            total = shared_part(
                share_ref,
                m_refs,
                part_ref[...],
                lambda p, s: mine_ref[p * slots + s],
                lambda p, s: their_refs[p][p * slots + s],
                slot_reader(s0, s1),
                v_ref,
                x_ref,
                u_ref,
                z_ref,
            )
            for k in range(owned):
                h_ref[k] = total[:, k * block : (k + 1) * block].astype(BF16)
            gram = nt(total, jnp.concatenate([wide(b_ref), wide(u_ref), total], axis=0))
            for e, part in enumerate(cut3(padded(gram * weighting))):
                h_ref[owned + e] = part

        outs = (sds((owned + EXTRA, cases, block), BF16), sds(cube))
        args = (share, part, base, *slot_inv, v, x, mine, *matrix, *theirs)
        return call(
            kernel, outs, args, [SM] + [VM] * (len(args) - 1), scratch=[pltpu.VMEM(cube, F32)], vmem=16, name="tail_second"
        )

    def gram_and_cross(g_ref, s_ref, theirs, all_ref):
        gram = pair_sum([g_ref[...]] + [join3([r[n_slots + e] for e in range(EXTRA)]) for r in theirs])
        all_ref[me_sub()] = s_ref[...]
        for m, t_ref in zip(peers, theirs):
            all_ref[me_sub() ^ m] = t_ref[...]
        cross = jnp.zeros((n, n), F32)
        for i in range(subs):
            for j in range(i + 1, subs):
                at = ((i ^ j) - 1) * slots
                left = jnp.concatenate([all_ref[i, at + s] for s in range(slots)], axis=1)
                right = jnp.concatenate([all_ref[j, at + s] for s in range(slots)], axis=1)
                cross = cross + nt16(left, right)
        return gram, (cross + cross.T) * weighting

    def early(g01, mine, theirs):
        def kernel(g_ref, s_ref, *rest):
            ins, (u00_ref, i00_ref, l10_ref, u11_ref, i11_ref, j1_ref, r1_ref, all_ref) = rest[:n_in], rest[n_in:]
            g, cross = gram_and_cross(g_ref, s_ref, ins, all_ref)
            g00, g10, g11 = g[:, :n], g[:, n : 2 * n], g[:, 2 * n : 3 * n] + cross
            (u00, i00), (_, j1) = factor([g00, g11])
            l10 = nt(g10, i00)
            ((u11, i11),) = factor([g11 - nt(l10, l10)])
            u00_ref[...] = u00
            i00_ref[...] = i00
            l10_ref[...] = l10
            u11_ref[...] = u11
            i11_ref[...] = i11
            j1_ref[...] = j1
            r1_ref[...] = nt(g10.T, j1)

        outs = tuple(sds((n, n)) for _ in range(7))
        cost = pl.CostEstimate(flops=10**8, transcendentals=0, bytes_accessed=10**7)
        return call(
            kernel,
            outs,
            (g01, mine, *theirs),
            [VM] * (2 + n_in),
            scratch=[pltpu.VMEM((subs,) + mine.shape, BF16)],
            vmem=24,
            name="early",
            cost=cost,
        )

    def finish(g2, mine, theirs, known, upper, inv_low, z0, z1):
        n_known = len(known)

        def kernel(g_ref, s_ref, f_ref, t_ref, z0_ref, z1_ref, *rest):
            known_refs, rest = rest[:n_known], rest[n_known:]
            ins, (sol_ref, mis_ref, all_ref) = rest[:n_in], rest[n_in:]
            u00, i00, l10, u11, i11, j1, r1 = (r[...] for r in known_refs)
            g, cross = gram_and_cross(g_ref, s_ref, ins, all_ref)
            g20, g21, g22 = g[:, :n], g[:, n : 2 * n], g[:, 2 * n : 3 * n] + cross
            l20 = nt(g20, i00)
            k21 = nt(g21, j1)
            l21 = nt(g21 - nt(l20, l10), i11)
            (u22, _), (_, j2) = factor([g22 - nt(l20, l20) - nt(l21, l21), g22 - nt(k21, k21)])
            r2 = nt(g20.T - nt(r1, k21), j2)
            c1 = nn(r2, j2)
            c0 = nn(r1 - nn(c1, k21), j1)
            low = f_ref[...].T
            m0 = u00.T - nn(c0, l10) - nn(c1, l20)
            m1 = -nt(c0, u11) - nn(c1, l21)
            m2 = -nt(c1, u22)
            mixed = nn(low, jnp.concatenate([m0, m1, m2, nn(c0, t_ref[...]), c1], axis=1))
            mis_ref[...] = mixed[:, : 3 * n]
            both = mixed[:, 3 * n :]
            for k in range(owned):
                z = jnp.concatenate([z0_ref[k], z1_ref[k]], axis=0)
                sol_ref[:, k * block : (k + 1) * block] = nn(both, z)

        outs = (sds((n, local_rows)), sds((n, 3 * n)))
        return call(
            kernel,
            outs,
            (g2, mine, upper, inv_low, z0, z1, *known, *theirs),
            [VM] * (6 + n_known + n_in),
            scratch=[pltpu.VMEM((subs,) + mine.shape, BF16)],
            vmem=24,
            name="finish",
        )

    def rest_of(matrix, pieces, stride, part):
        first = pieces[0].shape[0] // stride
        for p in pieces[1:]:
            part = multiply(matrix, p, first, stride, part)
        return part

    v0, x0, half = open_(loads[0])
    slot_inv, lent, gate, late = slot_inverse(v0)
    matrix, touched = lax.optimization_barrier((schur[0], touch(schur[0], lent)))
    matrix = [matrix]
    pieces, part = gather(half, lambda p: multiply(matrix, p, 0, owned + 1, None), gate)
    mine = select_first(pieces, late)
    theirs = to_subs(mine)
    part = rest_of(matrix, pieces, owned + 1, part)
    v1, half, x1, b, z0, upper, inv_low = tail_first(matrix, part, mine, theirs, slot_inv, v0, x0)

    pieces, part = gather(half, lambda p: multiply(matrix, p, 0, owned + EXTRA, None))
    mine, g01 = select(pieces, True, part)
    theirs = to_subs([mine] * n_in)
    part = rest_of(matrix, pieces, owned + EXTRA, part)
    half, z1 = tail_second(matrix, part, mine, theirs, slot_inv, v1, x1, b)

    pieces, known = gather(half, lambda p: early(g01, mine, theirs))
    mine, g2 = select(pieces, True, known[0])
    solution, misfit = finish(g2, mine, to_subs([mine] * n_in), known, upper, inv_low, z0, z1)
    return (solution[None], misfit)


def solution(mesh):
    placed = (
        P("sub", "blk", None),
        P("sub", "blk", None, None),
        P("sub", None, "blk"),
        P("sub", None, None),
        P("sub", "blk"),
    )
    return jax.shard_map(
        body, mesh=mesh, in_specs=placed, out_specs=(P("sub", None, "blk"), P()), check_vma=False
    )
```

```python
import functools

import jax
import jax.numpy as jnp
from jax import lax
from jax.experimental import pallas as pl
from jax.experimental.pallas import tpu as pltpu
from jax.sharding import PartitionSpec as P


F32 = jnp.float32
BF16 = jnp.bfloat16
HIGH = lax.Precision.HIGHEST
VM = pl.BlockSpec(memory_space=pltpu.VMEM)
SM = pl.BlockSpec(memory_space=pltpu.SMEM)


def nn(a, b):
    return lax.dot_general(a, b, (((1,), (0,)), ((), ())), precision=HIGH, preferred_element_type=F32)


def nt(a, b):
    return lax.dot_general(a, b, (((1,), (1,)), ((), ())), precision=HIGH, preferred_element_type=F32)


def nt16(a, b):
    return lax.dot_general(a, b, (((1,), (1,)), ((), ())), preferred_element_type=F32)


def pair_sum(values):
    while len(values) > 1:
        values = [values[i] + values[i + 1] for i in range(0, len(values), 2)]
    return values[0]


def factor(mats, group=8):
    size = mats[0].shape[0]
    rows = lax.broadcasted_iota(jnp.int32, (size, size), 0)
    cols = lax.broadcasted_iota(jnp.int32, (size, size), 1)
    eye = (rows == cols).astype(F32)
    work = [jnp.concatenate([m, eye], axis=1) for m in mats]
    kept = [[] for _ in mats]
    pivots = [[] for _ in mats]
    for first in range(0, size, group):
        last = min(first + group, size)
        spread = [[jnp.broadcast_to(m[:, j : j + 1], m.shape) for j in range(first, last)] for m in work]
        for j in range(first, last):
            for i in range(len(mats)):
                col = spread[i][j - first]
                pivot, row = col[j : j + 1, :], work[i][j : j + 1, :]
                kept[i].append(row)
                pivots[i].append(pivot)
                over = 1.0 / pivot
                for c in range(j + 1 - first, last - first):
                    other = spread[i][c]
                    spread[i][c] = other - col * (other[j : j + 1, :] * over)
                work[i] = work[i] - col * (row * over)
    out = []
    for i in range(len(mats)):
        full = jnp.concatenate(kept[i], axis=0) * lax.rsqrt(jnp.concatenate(pivots[i], axis=0))
        out.append((jnp.where(cols >= rows, full[:, :size], 0.0), full[:, size:]))
    return out


def cut3(v):
    high = v.astype(BF16)
    rest = v - high.astype(F32)
    mid = rest.astype(BF16)
    return high, mid, (rest - mid.astype(F32)).astype(BF16)


def join3(parts):
    high, mid, low = (p.astype(F32) for p in parts)
    return high + (mid + low)


def call(kernel, outs, args, specs, scratch=(), vmem=8, name=None, cost=None, spaces=None):
    return pl.pallas_call(
        kernel,
        out_shape=outs,
        in_specs=specs,
        out_specs=jax.tree.map(lambda _: VM, outs) if spaces is None else spaces,
        scratch_shapes=list(scratch),
        compiler_params=pltpu.CompilerParams(vmem_limit_bytes=vmem << 20),
        cost_estimate=cost,
        name=name,
    )(*args)


def xor(size, m):
    return [(i, i ^ m) for i in range(size)]


EXTRA = 3
CHUNKS = 1


def body(schur, inverse_blocks, loads, share_list, multiplicity):
    inverse = inverse_blocks[0]
    local_rows, order = schur.shape[1:]
    owned, block = inverse.shape[0], inverse.shape[-1]
    cases = loads.shape[1]
    share = share_list[0]
    subs, slots = share.shape
    parts = lax.axis_size("blk")
    zs = parts // 2
    weighting = 1.0 / (order * subs)
    blocks = order // block
    peers = list(range(1, subs))
    n_in = len(peers)
    n_slots = n_in * slots
    cube = (owned, cases, block)
    unit = (block // 2, block)
    per = -(-2 * n_slots // parts)
    n = cases

    def sds(shape, dtype=F32):
        return jax.ShapeDtypeStruct(shape, dtype)

    def permute(v, axis, m):
        return lax.ppermute(v, axis, xor(lax.axis_size(axis), m))

    def to_subs(vs):
        return [permute(v, "sub", m) for m, v in zip(peers, vs)]

    def padded(v):
        if v.shape[1] == block:
            return v
        return jnp.concatenate([v, jnp.zeros((v.shape[0], block - v.shape[1]), v.dtype)], axis=1)

    def me_blk():
        return lax.axis_index("blk")

    def me_sub():
        return lax.axis_index("sub")

    def wide(ref):
        return jnp.concatenate([ref[k] for k in range(owned)], axis=1)

    def weighted(ref, plain_ref):
        one = lambda k: jnp.where(plain_ref[me_blk() * owned + k] > 0, 1.0, 0.5)
        return jnp.concatenate([ref[k] * one(k) for k in range(owned)], axis=1)

    anywhere = pl.BlockSpec(memory_space=pl.ANY)

    def far_and_self(v):
        far = {m: permute(v, "blk", 2 * m) for m in reversed(range(1, zs))}
        far[0] = v
        return [far[m] for m in range(zs)]


    def slot_inverse(lent, after):
        arrived = to_subs(lent)

        def deal(*refs):
            mine, theirs, (_, keep_ref, send_ref, all_ref) = refs[:n_in], refs[n_in : 2 * n_in], refs[2 * n_in :]
            me = me_blk()
            for i in range(n_slots):
                p, s = i // slots, i % slots
                value = mine[p][s].astype(F32) + theirs[p][s].astype(F32)
                for h in range(2):
                    u = 2 * i + h
                    all_ref[u // per, u % per] = value[h * unit[0] : (h + 1) * unit[0]]
            for u in range(2 * n_slots, parts * per):
                all_ref[u // per, u % per] = jnp.zeros(unit, F32)
            for q in range(zs):
                keep_ref[q] = all_ref[me ^ (2 * q)].astype(BF16)
                send_ref[q] = all_ref[me ^ (2 * q + 1)].astype(BF16)

        shape = (zs, per) + unit
        keep, send = call(
            deal,
            (sds(shape, BF16), sds(shape, BF16)),
            (*lent, *arrived, after),
            [VM] * (2 * n_in) + [anywhere],
            scratch=[pltpu.VMEM((parts, per) + unit, F32)],
            vmem=16,
            name="deal",
        )
        return keep + permute(send, "blk", 1)

    def slot_reduce(keep):
        far = [permute(keep[m], "blk", 2 * m) for m in reversed(range(1, zs))]
        return pair_sum([v.astype(F32) for v in [keep[0]] + far[::-1]]).astype(BF16)

    def slot_gather(mine, work):
        pieces, done = lax.optimization_barrier((far_and_self(mine), work))
        same = jnp.stack(pieces)
        return (same, permute(same, "blk", 1)), done

    def slot_reader(same_ref, other_ref):
        def unit_at(u):
            q = (u // per) ^ me_blk()
            value, other = same_ref[q // 2, u % per], other_ref[q // 2, u % per]
            return jnp.where(q % 2 == 0, value, other)

        return lambda i: jnp.concatenate([unit_at(2 * i), unit_at(2 * i + 1)], axis=0)


    def gather(v, work):
        pieces = far_and_self(v)
        if work is None:
            far = [w for p in pieces for w in (p, permute(p, "blk", 1))]
            return [jnp.concatenate(far[:4], axis=0)] + ([jnp.concatenate(far[4:], axis=0)] if far[4:] else []), None
        near, far = pieces[:1], pieces[1:]
        near = jnp.concatenate([w for p in near for w in (p, permute(p, "blk", 1))], axis=0)
        done = work(near)
        if not far:
            return [near], done
        far, done = lax.optimization_barrier((far, done))
        far = jnp.concatenate([w for p in far for w in (p, permute(p, "blk", 1))], axis=0)
        return [near, far], done

    def piece_reader(p_refs, stride):
        sizes = [r.shape[0] // stride for r in p_refs]

        def read(k):
            q, r = (k // owned) ^ me_blk(), k % owned
            value = p_refs[0][jnp.minimum(q, sizes[0] - 1) * stride + r]
            if len(p_refs) > 1:
                other = p_refs[1][jnp.maximum(q - sizes[0], 0) * stride + r]
                value = jnp.where(q < sizes[0], value, other)
            return value

        return read

    def extra_sum(p_refs, stride):
        found = []
        for r in p_refs:
            for q in range(r.shape[0] // stride):
                found.append(join3([r[q * stride + owned + e] for e in range(EXTRA)]))
        return pair_sum(found)

    def select_first(pieces, after):
        stride, n_p = owned + 1, len(pieces)

        def kernel(share_ref, after_ref, *refs):
            p_refs, outs = refs[:n_p], refs[n_p:]
            read = piece_reader(p_refs, stride)
            for i in range(n_slots):
                k = share_ref[me_sub() ^ peers[i // slots], i % slots]
                value = read(jnp.maximum(k, 0))
                outs[i // slots][i % slots] = jnp.where(k >= 0, value, jnp.zeros_like(value))
            total = pair_sum([r[q * stride + owned] for r in p_refs for q in range(r.shape[0] // stride)])
            for o_ref in outs:
                o_ref[slots] = total

        outs = tuple(sds((slots + 1, cases, block)) for _ in peers)
        return call(kernel, outs, (share, after, *pieces), [SM, anywhere] + [VM] * n_p, name="select_first")

    def select(pieces, extra, after):
        stride = owned + (EXTRA if extra else 0)
        n_p = len(pieces)
        more = EXTRA if extra else 0

        def kernel(share_ref, after_ref, *refs):
            p_refs, outs = refs[:n_p], refs[n_p:]
            read = piece_reader(p_refs, stride)
            for i in range(n_slots):
                k = share_ref[me_sub() ^ peers[i // slots], i % slots]
                value = read(jnp.maximum(k, 0))
                value = jnp.where(k >= 0, value, jnp.zeros_like(value))
                if extra:
                    outs[0][i] = value
                else:
                    outs[i // slots][i % slots] = value
            if extra:
                total = extra_sum(p_refs, stride)
                outs[-1][...] = total
                for e, part in enumerate(cut3(total)):
                    outs[0][n_slots + e] = part

        if extra:
            outs = (sds((n_slots + more, cases, block), BF16), sds((cases, block)))
        else:
            outs = tuple(sds((slots, cases, block), BF16) for _ in peers)
        return call(kernel, outs, (share, after, *pieces), [SM, anywhere] + [VM] * n_p, name="select")


    def mix(plain_ref, inv_ref, v_ref, x_ref, h_ref):
        for k in range(owned):
            value = v_ref[k]
            x = nt(value, inv_ref[k])
            x_ref[k] = x
            h_ref[k] = jnp.where(plain_ref[me_blk() * owned + k] > 0, x, value).astype(h_ref.dtype)

    def open_(raw):
        def kernel(share_ref, l_ref, inv_ref, v_ref, x_ref, h_ref, plain_ref, *lent):
            for k in range(blocks):
                plain_ref[k] = 1
            for m, o_ref in zip(peers, lent):
                for s in range(slots):
                    at = share_ref[me_sub() ^ m, s]

                    @pl.when(at >= 0)
                    def _():
                        plain_ref[at] = 0

                    here = jnp.logical_and(at >= 0, at // owned == me_blk())
                    o_ref[s] = jnp.where(here, 0.5 * inv_ref[jnp.where(here, at % owned, 0)], 0.0).astype(BF16)
            value = l_ref[...]
            for k in range(owned):
                v_ref[k] = value[:, k * block : (k + 1) * block]
            mix(plain_ref, inv_ref, v_ref, x_ref, h_ref)
            h_ref[owned] = padded(nt(value, value) * weighting)

        outs = (sds(cube), sds(cube), sds((owned + 1, cases, block)), sds((blocks,), jnp.int32))
        outs += tuple(sds((slots, block, block), BF16) for _ in peers)
        return call(
            kernel, outs, (share, raw, inverse), [SM, VM, VM], name="open", spaces=(VM, VM, VM, SM) + (VM,) * n_in
        )

    def touch(full, after):
        def kernel(m_ref, a_ref, o_ref):
            o_ref[...] = m_ref[:8, :block].astype(F32)

        return call(kernel, sds((8, block)), (full, after), [VM, anywhere], name="touch")

    def multiply(matrix, pieces, first, stride, before, after=None):
        count = pieces.shape[0] // stride
        wide_type = pieces.dtype == F32
        rows = local_rows // CHUNKS

        def kernel(plain_ref, p_ref, after_ref, *rest):
            m_refs, y_ref = rest[:CHUNKS], rest[-1]
            totals = [
                rest[CHUNKS][:, c * rows : (c + 1) * rows] if before is not None else jnp.zeros((n, rows), F32)
                for c in range(CHUNKS)
            ]
            for q in range(count):
                owner = (first + q) ^ me_blk()
                z = []
                for i in range(owned):
                    value = p_ref[q * stride + i]
                    z.append(jnp.where(plain_ref[owner * owned + i] > 0, value, jnp.zeros_like(value)))
                z = jnp.concatenate(z, axis=1)
                if wide_type:
                    high = z.astype(BF16)
                    z = jnp.concatenate([high, (z - high.astype(F32)).astype(BF16)], axis=0)
                at = pl.multiple_of(owner * local_rows, local_rows)
                for c in range(CHUNKS):
                    found = nt16(z, m_refs[c][:, pl.ds(at, local_rows)])
                    totals[c] = totals[c] + (found[:n] + found[n:] if wide_type else found)
            for c in range(CHUNKS):
                y_ref[:, c * rows : (c + 1) * rows] = totals[c]

        args = (plain, pieces, share if after is None else after, *matrix) + (() if before is None else (before,))
        cost = pl.CostEstimate(
            flops=2 * n * local_rows * local_rows * count,
            transcendentals=0,
            bytes_accessed=2 * local_rows * local_rows * count,
        )
        return call(kernel, sds((n, local_rows)), args, [SM, VM, anywhere] + [VM] * (len(args) - 3), name="multiply", cost=cost)

    def shared_part(share_ref, m_refs, total, mine, theirs, inv_at, v_ref, x_ref, u_ref, z_ref):
        u_ref[...] = v_ref[...]
        z_ref[...] = x_ref[...]
        totals = [total[:, c * (local_rows // CHUNKS) : (c + 1) * (local_rows // CHUNKS)] for c in range(CHUNKS)]
        for p, m in enumerate(peers):
            zz, where_ = [], []
            for s in range(slots):
                k = share_ref[me_sub() ^ m, s]
                far = theirs(p, s)
                near = mine(p, s)
                if far.dtype == F32:
                    both = near + far
                    near = both.astype(BF16)
                    lower = (both - near.astype(F32)).astype(BF16)
                else:
                    lower = far
                both = nt16(jnp.concatenate([near, lower], axis=0), inv_at(p * slots + s))
                both = both[:n] + both[n:]
                high = both.astype(BF16)
                if far.dtype == F32:
                    high = jnp.concatenate([high, (both - high.astype(F32)).astype(BF16)], axis=0)
                zz.append(high)
                where_.append(pl.multiple_of(jnp.maximum(k, 0) * block, block))

                @pl.when(jnp.logical_and(k >= 0, k // owned == me_blk()))
                def _():
                    u_ref[k % owned] += far.astype(F32)
                    z_ref[k % owned] = both

            zz = jnp.concatenate(zz, axis=1)
            for c in range(CHUNKS):
                cols = jnp.concatenate([m_refs[c][:, pl.ds(at, block)] for at in where_], axis=1)
                found = nt16(zz, cols)
                totals[c] = totals[c] + (found[:n] + found[n:] if found.shape[0] > n else found)
        return jnp.concatenate(totals, axis=1)

    def tail_first(matrix, part, mine, theirs, slot_inv, v, x):
        def kernel(share_ref, plain_ref, part_ref, inv_ref, s0, s1, v_ref, x_ref, *rest):
            m_refs, rest = rest[:CHUNKS], rest[CHUNKS:]
            mine_refs, their_refs, (y_ref, h_ref, x1_ref, u_ref, z_ref, f_ref, i_ref) = (
                rest[:n_in],
                rest[n_in : 2 * n_in],
                rest[2 * n_in :],
            )
            total = shared_part(
                share_ref,
                m_refs,
                part_ref[...],
                lambda p, s: mine_refs[p][s],
                lambda p, s: their_refs[p][s],
                slot_reader(s0, s1),
                v_ref,
                x_ref,
                u_ref,
                z_ref,
            )
            grams = [mine_refs[0][slots]] + [r[slots] for r in their_refs]
            ((up, inv_low),) = factor([pair_sum(grams)[:, :n]])
            f_ref[...] = up
            i_ref[...] = inv_low
            total = nn(inv_low, jnp.concatenate([total, wide(u_ref)], axis=1))
            total, base = total[:, :local_rows], total[:, local_rows:]
            for k in range(owned):
                y_ref[k] = total[:, k * block : (k + 1) * block]
                u_ref[k] = base[:, k * block : (k + 1) * block]
            mix(plain_ref, inv_ref, y_ref, x1_ref, h_ref)
            g0 = nt(weighted(u_ref, plain_ref), base)
            g1 = nt(total, jnp.concatenate([base, total], axis=0))
            gram = padded(jnp.concatenate([g0, g1], axis=1) * weighting)
            for e, part in enumerate(cut3(gram)):
                h_ref[owned + e] = part

        outs = (sds(cube), sds((owned + EXTRA, cases, block), BF16)) + (sds(cube),) * 3 + (sds((n, n)),) * 2
        args = (share, plain, part, inverse, *slot_inv, v, x, *matrix, *mine, *theirs)
        return call(kernel, outs, args, [SM] * 2 + [VM] * (len(args) - 2), vmem=16, name="tail_first")

    def tail_second(matrix, part, mine, theirs, slot_inv, v, x, base):
        def kernel(share_ref, part_ref, b_ref, s0, s1, v_ref, x_ref, mine_ref, *rest):
            m_refs, rest = rest[:CHUNKS], rest[CHUNKS:]
            their_refs, (h_ref, z_ref, u_ref) = rest[:n_in], rest[n_in:]
            total = shared_part(
                share_ref,
                m_refs,
                part_ref[...],
                lambda p, s: mine_ref[p * slots + s],
                lambda p, s: their_refs[p][p * slots + s],
                slot_reader(s0, s1),
                v_ref,
                x_ref,
                u_ref,
                z_ref,
            )
            for k in range(owned):
                h_ref[k] = total[:, k * block : (k + 1) * block].astype(BF16)
            gram = nt(total, jnp.concatenate([wide(b_ref), wide(u_ref), total], axis=0))
            for e, part in enumerate(cut3(padded(gram * weighting))):
                h_ref[owned + e] = part

        outs = (sds((owned + EXTRA, cases, block), BF16), sds(cube))
        args = (share, part, base, *slot_inv, v, x, mine, *matrix, *theirs)
        return call(
            kernel, outs, args, [SM] + [VM] * (len(args) - 1), scratch=[pltpu.VMEM(cube, F32)], vmem=16, name="tail_second"
        )

    def gram_and_cross(g_ref, s_ref, theirs, all_ref):
        gram = pair_sum([g_ref[...]] + [join3([r[n_slots + e] for e in range(EXTRA)]) for r in theirs])
        all_ref[me_sub()] = s_ref[...]
        for m, t_ref in zip(peers, theirs):
            all_ref[me_sub() ^ m] = t_ref[...]
        cross = jnp.zeros((n, n), F32)
        for i in range(subs):
            for j in range(i + 1, subs):
                at = ((i ^ j) - 1) * slots
                left = jnp.concatenate([all_ref[i, at + s] for s in range(slots)], axis=1)
                right = jnp.concatenate([all_ref[j, at + s] for s in range(slots)], axis=1)
                cross = cross + nt16(left, right)
        return gram, (cross + cross.T) * weighting

    def early(g01, mine, theirs):
        def kernel(g_ref, s_ref, *rest):
            ins, (u00_ref, i00_ref, l10_ref, u11_ref, i11_ref, j1_ref, r1_ref, all_ref) = rest[:n_in], rest[n_in:]
            g, cross = gram_and_cross(g_ref, s_ref, ins, all_ref)
            g00, g10, g11 = g[:, :n], g[:, n : 2 * n], g[:, 2 * n : 3 * n] + cross
            (u00, i00), (_, j1) = factor([g00, g11])
            l10 = nt(g10, i00)
            ((u11, i11),) = factor([g11 - nt(l10, l10)])
            u00_ref[...] = u00
            i00_ref[...] = i00
            l10_ref[...] = l10
            u11_ref[...] = u11
            i11_ref[...] = i11
            j1_ref[...] = j1
            r1_ref[...] = nt(g10.T, j1)

        outs = tuple(sds((n, n)) for _ in range(7))
        cost = pl.CostEstimate(flops=10**8, transcendentals=0, bytes_accessed=10**7)
        return call(
            kernel,
            outs,
            (g01, mine, *theirs),
            [VM] * (2 + n_in),
            scratch=[pltpu.VMEM((subs,) + mine.shape, BF16)],
            vmem=24,
            name="early",
            cost=cost,
        )

    def finish(g2, mine, theirs, known, upper, inv_low, z0, z1):
        n_known = len(known)

        def kernel(g_ref, s_ref, f_ref, t_ref, z0_ref, z1_ref, *rest):
            known_refs, rest = rest[:n_known], rest[n_known:]
            ins, (sol_ref, mis_ref, all_ref) = rest[:n_in], rest[n_in:]
            u00, i00, l10, u11, i11, j1, r1 = (r[...] for r in known_refs)
            g, cross = gram_and_cross(g_ref, s_ref, ins, all_ref)
            g20, g21, g22 = g[:, :n], g[:, n : 2 * n], g[:, 2 * n : 3 * n] + cross
            l20 = nt(g20, i00)
            k21 = nt(g21, j1)
            l21 = nt(g21 - nt(l20, l10), i11)
            (u22, _), (_, j2) = factor([g22 - nt(l20, l20) - nt(l21, l21), g22 - nt(k21, k21)])
            r2 = nt(g20.T - nt(r1, k21), j2)
            c1 = nn(r2, j2)
            c0 = nn(r1 - nn(c1, k21), j1)
            low = f_ref[...].T
            m0 = u00.T - nn(c0, l10) - nn(c1, l20)
            m1 = -nt(c0, u11) - nn(c1, l21)
            m2 = -nt(c1, u22)
            mixed = nn(low, jnp.concatenate([m0, m1, m2, nn(c0, t_ref[...]), c1], axis=1))
            mis_ref[...] = mixed[:, : 3 * n]
            both = mixed[:, 3 * n :]
            for k in range(owned):
                z = jnp.concatenate([z0_ref[k], z1_ref[k]], axis=0)
                sol_ref[:, k * block : (k + 1) * block] = nn(both, z)

        outs = (sds((n, local_rows)), sds((n, 3 * n)))
        return call(
            kernel,
            outs,
            (g2, mine, upper, inv_low, z0, z1, *known, *theirs),
            [VM] * (6 + n_known + n_in),
            scratch=[pltpu.VMEM((subs,) + mine.shape, BF16)],
            vmem=24,
            name="finish",
        )

    def rest_of(matrix, pieces, stride, part):
        first = pieces[0].shape[0] // stride
        for p in pieces[1:]:
            part = multiply(matrix, p, first, stride, part)
        return part

    v0, x0, half, plain, *lent = open_(loads[0])
    matrix, touched = lax.optimization_barrier((schur[0], touch(schur[0], v0)))
    matrix = [matrix]
    keep = slot_inverse(lent, touched)
    pieces, _ = gather(half, None)
    mine = select_first(pieces, v0)
    theirs = to_subs(mine)
    keep, mine = lax.optimization_barrier((keep, mine))
    reduced = slot_reduce(keep)
    part = multiply(matrix, pieces[0], 0, owned + 1, None, mine[0])
    reduced, part, theirs = lax.optimization_barrier((reduced, part, theirs))
    slot_inv, part = slot_gather(reduced, rest_of(matrix, pieces, owned + 1, part))
    v1, half, x1, b, z0, upper, inv_low = tail_first(matrix, part, mine, theirs, slot_inv, v0, x0)

    pieces, part = gather(half, lambda p: multiply(matrix, p, 0, owned + EXTRA, None))
    mine, g01 = select(pieces, True, part)
    theirs = to_subs([mine] * n_in)
    part = rest_of(matrix, pieces, owned + EXTRA, part)
    half, z1 = tail_second(matrix, part, mine, theirs, slot_inv, v1, x1, b)

    pieces, known = gather(half, lambda p: early(g01, mine, theirs))
    mine, g2 = select(pieces, True, known[0])
    solution, misfit = finish(g2, mine, to_subs([mine] * n_in), known, upper, inv_low, z0, z1)
    return (solution[None], misfit)


def solution(mesh):
    placed = (
        P("sub", "blk", None),
        P("sub", "blk", None, None),
        P("sub", None, "blk"),
        P("sub", None, None),
        P("sub", "blk"),
    )
    return jax.shard_map(
        body, mesh=mesh, in_specs=placed, out_specs=(P("sub", None, "blk"), P()), check_vma=False
    )
```
